256 devices in a mesh: expert: 32 (over z, x), col: 8 (over y, core).
Axes of the slice: x: 4, y: 4, z: 8, core: 2. Of those that a mesh axis runs over, the one named last changes fastest.
Arguments:
- tokens: bfloat16 [4096, 4096], P('expert', 'col'), may hold values from -6 to 6
- routes: int32 [4096, 8], P('expert'), may hold values from 0 to 63, all different within a row; in each aligned block of 128 rows (0 to 127, 128 to 255, ...) at most 24 rows name the same one
- route_weight: float32 [4096, 8], P('expert'), may hold values from 0.02 to 0.25
- language: int32 [4096], P('expert'), may hold values from 0 to 118
- lang_weight: float32 [119], replicated, may hold values from 0.01 to 0.1
- w_gate: bfloat16 [64, 1536, 4096], P('expert', 'col'), may hold values from -0.09375 to 0.09375
- w_up: bfloat16 [64, 1536, 4096], P('expert', 'col'), may hold values from -0.09375 to 0.09375
- w_down: bfloat16 [64, 1536, 4096], P('expert', None, 'col'), may hold values from -0.15625 to 0.15625
Outputs:
- layer_out: bfloat16 [4096, 4096], P('expert', 'col')
- gram: float32 [64, 1536, 1536], P('expert', 'col')
The draws below stay inside these ranges and needn't reach their ends.
Inputs may be any that keep to these rules, and one draw needn't show every extreme that they name: `routes`: each row names 8 different experts. In each aligned block of 128 rows no expert is named by more than 24 rows, a bound that some block reaches.
All inputs are finite; a program needn't handle non-finite values.
Results may differ from the reference program's by a relative error of at most 0.0063.
Values may be sent and summed in bfloat16 or wider, within the bound.
A program may use at most 128 MiB of HBM per device.

```python
import math
import jax
import jax.numpy as jnp
import numpy as np
from jax import lax

D = 4096
FF = 1536
TOPK = 8
LANGS = 119
TOK_DEV = 128
EXPERTS = 64
TOKENS = 4096
CAP = 24


def place_ends(values, stream_key, least, top_value):
    spot = [jax.random.randint(jax.random.fold_in(stream_key, axis), (), 0, length) for axis, length in enumerate(values.shape)]
    widest = values.shape.index(max(values.shape))
    beside = spot[:widest] + [(spot[widest] + 1) % values.shape[widest]] + spot[widest + 1:]
    return values.at[tuple(spot)].set(least).at[tuple(beside)].set(top_value)


def block_levels(own_key, dims, shards, low, largest):
    level = 1.0
    for axis_at, blocks in shards:
        steps = jax.random.uniform(jax.random.fold_in(jax.random.fold_in(own_key, 6), axis_at), (blocks,), jnp.float32, low / len(shards), largest / len(shards))
        level = level * jnp.repeat(jnp.exp(steps), dims[axis_at] // blocks).reshape((-1,) + (1,) * (len(dims) - 1 - axis_at))
    return level


def rank_bounds(amount, skew):
    weights = [(1 << 20) // math.isqrt(standing ** skew) + 1 for standing in range(1, amount + 1)]
    deviation = 1 + sum(weights) // (1 << 30)
    return np.cumsum(np.array([max(1, weight // deviation) for weight in weights]))


def ranked(rng, shape, count, lean):
    table = rank_bounds(count, lean)
    pick = jax.random.randint(jax.random.fold_in(rng, 1), shape, 0, int(table[count - 1]))
    standing = jnp.searchsorted(jnp.asarray(table, jnp.int32), pick, side="right")
    return jax.random.permutation(jax.random.fold_in(rng, 2), count)[standing].astype(jnp.int32)


def routed_block(stream_key, own, number, rows, number_of, top, bound, slope):
    order = jax.random.permutation(stream_key, number_of)
    crowded, ordinary = load_shares(number_of, rows * top, bound, slope, True), load_shares(number_of, rows * top, bound, slope, False)
    places = jnp.arange(number_of)

    def named(tallies, rotation):
        used = int((tallies > 0).sum())
        fixed = max(1, used // 4)
        shifted = fixed + (places - fixed + rotation * (used - fixed)) % max(1, number_of - fixed)
        return jnp.zeros((number_of,), jnp.int32).at[order[jnp.where(places < fixed, places, shifted)]].set(jnp.asarray(tallies, jnp.int32))

    tallies = jnp.where(number % 4 == 0, named(crowded, number // 4), named(ordinary, number - number // 4 - 1))
    mixed = jax.random.permutation(jax.random.fold_in(own, 3), number_of)
    source_of, sink = mixed[0:number_of // 2 * 2:2], mixed[1:number_of // 2 * 2:2]
    margin = jnp.minimum(tallies[source_of] - 1, bound - tallies[sink]) // 2
    margin = jnp.where((source_of == order[0]) | (sink == order[0]) | (tallies[sink] == 0), 0, jnp.maximum(margin, 0))
    shifted = jax.random.randint(jax.random.fold_in(own, 4), (number_of // 2,), 0, 1 << 20) % (margin + 1)
    tallies = tallies.at[source_of].add(-shifted).at[sink].add(shifted)
    members = jnp.searchsorted(jnp.cumsum(tallies), jnp.arange(rows * top), side="right").astype(jnp.int32)
    table = members.reshape(top, rows).T
    table = table[jax.random.permutation(jax.random.fold_in(own, 1), rows)]
    rotation = jax.random.randint(jax.random.fold_in(own, 2), (rows, 1), 0, top)
    return jnp.take_along_axis(table, (jnp.arange(top)[None, :] + rotation) % top, axis=1)


def load_shares(count, total, limit, lean, full):
    weights = [(1 << 20) // math.isqrt(standing ** lean) + 1 for standing in range(1, count + 1)]
    largest = limit if full else min(limit, max(-(-total // count), total * weights[0] // sum(weights)))
    least = 1 if total - largest >= count - 1 else 0
    given, surplus = [largest] + [least] * (count - 1), total - largest - least * (count - 1)
    while surplus > 0:
        movable = [i for i in range(1, count) if given[i] < largest] or [i for i in range(1, count) if given[i] < limit]
        mass, budget = sum([weights[i] for i in movable]), surplus
        for i in movable:
            extra = min(limit - given[i], max(1, budget * weights[i] // mass), surplus)
            given[i] = given[i] + extra
            surplus = surplus - extra
    return np.array(given)


def bell_draw(own_key, dims, deviation, most, pieces=(), held_as=jnp.bfloat16):
    entries = jax.random.normal(own_key, dims, jnp.float32) * deviation
    if len(pieces) > 0:
        entries = block_levels(own_key, dims, pieces, -0.22, 0.18) * entries
    return jnp.clip(entries, min=-most, max=most).astype(held_as)


def setup_inputs(seed: int = 0) -> dict:
    arg_keys = jax.random.split(jax.random.key(seed), 9)
    tokens = bell_draw(arg_keys[0], (TOKENS, D), 1.0, 6.0, ((0, 32), (1, 8)))
    routes_keys = jax.random.split(jax.random.fold_in(arg_keys[1], 1), TOKENS // TOK_DEV)
    routes_turns = jax.random.permutation(jax.random.fold_in(arg_keys[1], 3), TOKENS // TOK_DEV)
    routes = jax.vmap(lambda own, number: routed_block(jax.random.fold_in(arg_keys[1], 2), own, number, TOK_DEV, EXPERTS, TOPK, CAP, 2))(routes_keys, routes_turns).reshape((TOKENS, TOPK))
    route_weight = jnp.clip(0.02 + 0.23 * jax.random.uniform(arg_keys[2], (TOKENS, TOPK), jnp.float32) ** block_levels(arg_keys[2], (TOKENS, TOPK), ((0, 32),), -0.2, 0.2), 0.02, 0.25)
    language = place_ends(ranked(arg_keys[3], (TOKENS,), LANGS, 2), jax.random.fold_in(arg_keys[3], 3), 0, LANGS - 1).astype(jnp.int32)
    lang_weight = jnp.clip(jnp.exp(jax.random.uniform(arg_keys[4], (LANGS,), jnp.float32, math.log(0.01), math.log(0.1))), 0.01, 0.1)
    w_gate = bell_draw(arg_keys[5], (EXPERTS, FF, D), D ** -0.5, 0.09375, ((0, 32), (1, 8)))
    w_up = bell_draw(arg_keys[6], (EXPERTS, FF, D), D ** -0.5, 0.09375, ((0, 32), (1, 8)))
    w_down = bell_draw(arg_keys[7], (EXPERTS, FF, D), FF ** -0.5, 0.15625, ((0, 32), (2, 8)))
    return {"tokens": tokens, "routes": routes, "route_weight": route_weight, "language": language, "lang_weight": lang_weight, "w_gate": w_gate, "w_up": w_up, "w_down": w_down}


def reference(tokens, routes, route_weight, language, lang_weight, w_gate, w_up, w_down):
    count = tokens.shape[0]
    blocks = count // TOK_DEV
    calib = lang_weight[language].astype(jnp.bfloat16)
    token_ids = jnp.arange(count, dtype=jnp.int32).reshape(blocks, TOK_DEV)
    block_ids = jnp.arange(blocks, dtype=jnp.int32)[:, None]

    def one_expert(carry, packed):
        expert_id, gate_w, up_w, down_w = packed
        chosen = routes == expert_id
        hit_rows = jnp.any(chosen, axis=1).astype(jnp.int32)
        coef = jnp.sum(jnp.where(chosen, route_weight, jnp.zeros((), route_weight.dtype)), axis=1)
        hit_block = hit_rows.reshape(blocks, TOK_DEV)
        place = jnp.cumsum(hit_block, axis=1) - hit_block
        target = jnp.where(hit_block == 1, place, CAP).astype(jnp.int32)
        table = jnp.zeros((blocks, CAP + 1), jnp.int32).at[block_ids, target].set(token_ids)
        marks = jnp.zeros((blocks, CAP + 1), jnp.int32).at[block_ids, target].set(1)
        table = table[:, :CAP].reshape(-1)
        filled = marks[:, :CAP].reshape(-1) == 1
        rows = jnp.where(filled[:, None], tokens[table], jnp.zeros((), tokens.dtype))
        gate = jnp.dot(rows, gate_w.T, preferred_element_type=jnp.float32)
        upper = jnp.dot(rows, up_w.T, preferred_element_type=jnp.float32)
        hidden = (jax.nn.silu(gate) * upper).astype(jnp.bfloat16)
        row_cal = jnp.where(filled, calib[table], jnp.zeros((), calib.dtype))
        scaled = (row_cal[:, None].astype(jnp.float32) * hidden.astype(jnp.float32)).astype(jnp.bfloat16)
        gram = jnp.dot(scaled.T, hidden, preferred_element_type=jnp.float32)
        expert_out = jnp.dot(hidden, down_w, preferred_element_type=jnp.float32).astype(jnp.bfloat16)
        weight_rows = jnp.where(filled, coef[table], jnp.zeros((), coef.dtype))
        carry = carry.at[table].add(weight_rows[:, None] * expert_out.astype(jnp.float32))
        return carry, gram

    start = jnp.zeros((count, tokens.shape[1]), jnp.float32)
    expert_ids = jnp.arange(EXPERTS, dtype=jnp.int32)
    total, grams = lax.scan(one_expert, start, (expert_ids, w_gate, w_up, w_down))
    return total.astype(jnp.bfloat16), grams
```

```python
import jax
import jax.numpy as jnp
from jax import lax
from jax.experimental import pallas as pl
from jax.experimental.pallas import tpu as pltpu
from jax.sharding import PartitionSpec as P

MESH = pl.DeviceIdType.MESH
NZ, NX, NY = 8, 4, 4
TOK = 128
CAP = 24
PAIR = 2 * CAP
ROWS = NX * PAIR
CHUNKS = NZ // 2
D = 4096
DS = 512
FF = 1536
FS = 192
FC = 2 * FS
NSEM = 128

F32 = jnp.float32
BF16 = jnp.bfloat16


def kernel(
    tok_hbm, meta_hbm, wg_hbm, wu_hbm, wd_hbm,
    out_ref, gram_ref,
    tok, meta, pick_send, row_buf, cal_send, cal_buf, xs, w_in, w_dn,
    hid_own, scaled, hid, eo, back, coef_hi, coef_lo, part, part_in, gram,
    send_sem, recv_sem, local_sem,
):
    i = lax.axis_index("expert")
    c = lax.axis_index("col")
    z, x = i // NX, lax.rem(i, NX)
    y, k = c // 2, lax.rem(c, 2)
    other = 1 - k

    def at_z(step):
        return (lax.rem(z + step + NZ, NZ) * NX + x, c)

    def at_x(step, flip=0):
        core = other if flip else k
        return (z * NX + lax.rem(x + step + NX, NX), y * 2 + core)

    def at_y(step, flip=0):
        core = other if flip else k
        return (i, lax.rem(y + step + NY, NY) * 2 + core)

    sibling = (i, y * 2 + other)

    count = [0, 0]
    sent = []

    def remote(src, dst, device):
        n = count[0]
        count[0] += 1
        copy = pltpu.make_async_remote_copy(
            src_ref=src, dst_ref=dst, send_sem=send_sem.at[n], recv_sem=recv_sem.at[n],
            device_id=device, device_id_type=MESH,
        )
        copy.start()
        sent.append(copy)
        return copy

    def local(src, dst):
        n = count[1]
        count[1] += 1
        copy = pltpu.make_async_copy(src, dst, local_sem.at[n])
        copy.start()
        return copy

    def arrive(copies):
        for copy in copies:
            copy.wait_recv()

    own_tok = local(tok_hbm, tok.at[pl.ds(0, TOK), :])
    own_meta = local(meta_hbm, meta.at[0])
    own_rows = pl.ds(pl.multiple_of(k * FS, 64), FS)
    own_rows_up = pl.ds(pl.multiple_of(FC + k * FS, 64), FS)
    weights_local = [
        local(wg_hbm.at[k], w_in.at[own_rows, :]),
        local(wu_hbm.at[k], w_in.at[own_rows_up, :]),
        local(wd_hbm.at[k], w_dn.at[0]),
    ]

    barrier = pltpu.get_barrier_semaphore()
    partners = [at_z(s) for s in range(1, NZ)]
    partners += [at_x(s, f) for s in range(1, NX) for f in range(2)]
    partners += [at_y(s, f) for s in (-1, 1) for f in range(2)]
    partners += [sibling]
    for device in partners:
        pl.semaphore_signal(barrier, inc=1, device_id=device, device_id_type=MESH)
    pl.semaphore_wait(barrier, len(partners))

    def slot_of(offset):
        return 2 * offset if offset >= 0 else 2 * (-offset - 1) + 1

    def z_send(source, target, step):
        a, b = slot_of(source), slot_of(target)
        device = at_z(step)
        return [
            remote(tok.at[pl.ds(a * TOK, TOK), :], tok.at[pl.ds(b * TOK, TOK), :], device),
            remote(meta.at[a], meta.at[b], device),
        ]

    own_tok.wait()
    own_meta.wait()
    right = {1: z_send(0, -1, 1)}
    left = {1: z_send(0, 1, -1)}

    weights_remote = [
        remote(wg_hbm.at[other], w_in.at[own_rows, :], sibling),
        remote(wu_hbm.at[other], w_in.at[own_rows_up, :], sibling),
        remote(wd_hbm.at[other], w_dn.at[1], sibling),
    ]

    lane = lax.broadcasted_iota(jnp.int32, (2 * TOK, 2 * TOK), 1)
    sub = lax.broadcasted_iota(jnp.int32, (2 * TOK, 2 * TOK), 0)
    before = jnp.where((sub < lane) & (sub // TOK == lane // TOK), 1.0, 0.0).astype(BF16)
    block_base = jnp.where(
        lax.broadcasted_iota(jnp.int32, (1, 2 * TOK), 1) >= TOK, float(CAP), 0.0
    )
    row_id = lax.broadcasted_iota(jnp.int32, (PAIR, 2 * TOK), 0).astype(F32)

    picked, cal_in = {}, {}

    def stage_pick(p):
        arrive(right[p + 1])
        if p + 2 <= CHUNKS:
            right[p + 2] = z_send(-(p + 1), -(p + 2), 1)
        if p + 1 < CHUNKS:
            arrive(left[p + 1])
        if p + 2 < CHUNKS:
            left[p + 2] = z_send(p + 1, p + 2, -1)
        m0, m1 = meta[2 * p], meta[2 * p + 1]
        pair = jnp.concatenate([m0, m1], axis=1)
        experts, gains = pair[0:8], pair[8:16]
        cal = pair[16:17]
        hits, coefs = [], []
        for flip in range(2):
            for step in range(NX):
                e = (z * NX + lax.rem(x + step, NX)) * 2 + (other if flip else k)
                same = experts == e.astype(F32)
                hits.append(jnp.max(jnp.where(same, 1.0, 0.0), axis=0, keepdims=True))
                coefs.append(jnp.sum(jnp.where(same, gains, 0.0), axis=0, keepdims=True))
        hit = jnp.concatenate(hits, axis=0)
        place = jnp.dot(hit.astype(BF16), before, preferred_element_type=F32)
        where_to = jnp.where(hit > 0.5, place + block_base, -1.0)
        picks = []
        for g in range(2 * NX):
            mask = row_id == where_to[g : g + 1]
            picks.append(jnp.where(mask, 1.0, 0.0).astype(BF16))
            high = coefs[g].astype(BF16).astype(F32)
            coef_hi[p, pl.ds(g * PAIR, PAIR), :] = jnp.where(mask, high, 0.0).astype(BF16)
            coef_lo[p, pl.ds(g * PAIR, PAIR), :] = jnp.where(mask, coefs[g] - high, 0.0).astype(BF16)
            if g < NX:
                col = jnp.sum(jnp.where(mask, cal, 0.0), axis=1, keepdims=True)
                wide = jnp.broadcast_to(col, (PAIR, TOK)).astype(BF16)
                if g == 0:
                    cal_buf[pl.ds(p * ROWS, PAIR), :] = wide
                else:
                    cal_send[pl.ds(p * ROWS + g * PAIR, PAIR), :] = wide
        rows = jnp.dot(
            jnp.concatenate(picks, axis=0), tok[pl.ds(2 * p * TOK, 2 * TOK), :],
            preferred_element_type=F32,
        ).astype(BF16)
        for flip in range(2):
            mine = rows[flip * ROWS : (flip + 1) * ROWS]
            row_buf[flip, pl.ds(p * ROWS, PAIR), :] = mine[0:PAIR]
            pick_send[flip, pl.ds(p * ROWS, ROWS), :] = mine
        picked[p], cal_in[p] = [], []
        for step in range(1, NX):
            device = at_x(step)
            src = pl.ds(p * ROWS + step * PAIR, PAIR)
            dst = pl.ds(p * ROWS + (NX - step) * PAIR, PAIR)
            picked[p].append(remote(pick_send.at[:, src, :], row_buf.at[:, dst, :], device))
            cal_in[p].append(remote(cal_send.at[src, :], cal_buf.at[dst, :], device))

    own_lanes = pl.ds(pl.multiple_of(c * DS, DS), DS)
    own_hid = pl.ds(pl.multiple_of(y * FC, 128), FC)
    left_y, right_y = lax.rem(y + NY - 1, NY), lax.rem(y + 1, NY)
    direct, to_self, forwarded, kept = {}, {}, {}, {}

    def stage_spread(p):
        arrive(picked[p])
        rows = pl.ds(p * ROWS, ROWS)
        direct[p] = [
            remote(row_buf.at[flip, rows, :], xs.at[rows, own_lanes], at_y(step, flip))
            for flip in range(2) for step in (1, -1)
        ]
        to_self[p] = remote(row_buf.at[1, rows, :], xs.at[rows, own_lanes], sibling)
        kept[p] = local(row_buf.at[0, rows, :], xs.at[rows, own_lanes])

    def stage_forward(p):
        arrive(direct[p])
        half = ROWS // 2
        a = (pl.ds(p * ROWS, half), pl.ds(pl.multiple_of(left_y * 2 * DS, DS), 2 * DS))
        b = (pl.ds(p * ROWS + half, half), pl.ds(pl.multiple_of(right_y * 2 * DS, DS), 2 * DS))
        forwarded[p] = [
            remote(xs.at[a], xs.at[a], at_y(1)),
            remote(xs.at[b], xs.at[b], at_y(-1)),
        ]

    hid_direct, hid_forwarded, hid_kept = {}, {}, {}

    def stage_hidden(p):
        if p == 0:
            for copy in weights_local[:2]:
                copy.wait()
            arrive(weights_remote[:2])
        arrive(forwarded[p])
        to_self[p].wait_recv()
        kept[p].wait()
        arrive(cal_in[p])
        rows = pl.ds(p * ROWS, ROWS)
        both = lax.dot_general(
            xs[rows, :], w_in[...], (((1,), (1,)), ((), ())), preferred_element_type=F32
        )
        gate, up = both[:, 0:FC], both[:, FC : 2 * FC]
        h = (gate / (1.0 + jnp.exp(-gate)) * up).astype(BF16)
        hid_own[rows, :] = h
        hid_direct[p] = [
            remote(hid_own.at[rows, :], hid.at[rows, own_hid], at_y(step)) for step in (1, -1)
        ]
        hid_kept[p] = local(hid_own.at[rows, :], hid.at[rows, own_hid])
        cal = cal_buf[rows, :][:, 0:1].astype(F32)
        scaled[rows, :] = (cal * h.astype(F32)).astype(BF16)

    def stage_hidden_forward(p):
        arrive(hid_direct[p])
        half = ROWS // 2
        a = (pl.ds(p * ROWS, half), pl.ds(pl.multiple_of(left_y * FC, 128), FC))
        b = (pl.ds(p * ROWS + half, half), pl.ds(pl.multiple_of(right_y * FC, 128), FC))
        hid_forwarded[p] = [
            remote(hid.at[a], hid.at[a], at_y(1)),
            remote(hid.at[b], hid.at[b], at_y(-1)),
        ]

    returned, back_kept = {}, {}

    def stage_down(p):
        if p == 0:
            weights_local[2].wait()
            arrive(weights_remote[2:])
        arrive(hid_forwarded[p])
        hid_kept[p].wait()
        rows = pl.ds(p * ROWS, ROWS)
        for flip in range(2):
            eo[flip, rows, :] = jnp.dot(
                hid[rows, :], w_dn[flip], preferred_element_type=F32
            ).astype(BF16)
        returned[p] = []
        for step in range(NX):
            src = pl.ds(p * ROWS + step * PAIR, PAIR)
            dst = pl.ds(p * ROWS + (NX - step) % NX * PAIR, PAIR)
            for flip in range(2):
                if step == 0 and flip == 0:
                    back_kept[p] = local(eo.at[0, src, :], back.at[0, dst, :])
                else:
                    returned[p].append(
                        remote(eo.at[flip, src, :], back.at[flip, dst, :], at_x(step, flip))
                    )

    parts = []

    def stage_combine(p):
        arrive(returned[p])
        back_kept[p].wait()
        rows = back[:, pl.ds(p * ROWS, ROWS), :].reshape(2 * ROWS, DS)
        dims = (((0,), (0,)), ((), ()))
        total = lax.dot_general(coef_hi[p], rows, dims, preferred_element_type=F32)
        total = total + lax.dot_general(coef_lo[p], rows, dims, preferred_element_type=F32)
        part[pl.ds(2 * p * TOK, 2 * TOK), :] = total.astype(BF16)
        for b in range(2):
            if p == 0 and b == 0:
                continue
            s = pl.ds((2 * p + b) * TOK, TOK)
            offset = p if b == 0 else -(p + 1)
            parts.append(remote(part.at[s, :], part_in.at[s, :], at_z(offset)))

    grams = []

    def stage_gram():
        gram[...] = lax.dot_general(
            scaled[...], hid[...], (((0,), (0,)), ((), ())), preferred_element_type=F32
        )
        mine = pl.ds(pl.multiple_of(k * FS, 64), FS)
        theirs = pl.ds(pl.multiple_of(other * FS, 64), FS)
        grams.append(remote(gram.at[theirs, :], gram_ref.at[k], sibling))
        grams.append(local(gram.at[mine, :], gram_ref.at[k]))

    stage_pick(0)
    stage_pick(1)
    stage_spread(0)
    stage_pick(2)
    stage_spread(1)
    stage_pick(3)
    stage_forward(0)
    stage_spread(2)
    stage_forward(1)
    stage_hidden(0)
    stage_spread(3)
    stage_forward(2)
    stage_hidden_forward(0)
    stage_hidden(1)
    stage_down(0)
    stage_forward(3)
    stage_hidden_forward(1)
    stage_hidden(2)
    stage_combine(0)
    stage_down(1)
    stage_hidden_forward(2)
    stage_hidden(3)
    stage_combine(1)
    stage_down(2)
    stage_hidden_forward(3)
    stage_combine(2)
    stage_down(3)
    stage_gram()
    stage_combine(3)

    total = part[pl.ds(0, TOK), :].astype(F32)
    for n, copy in enumerate(parts):
        copy.wait_recv()
        total = total + part_in[pl.ds((n + 1) * TOK, TOK), :].astype(F32)
    out_ref[...] = total.astype(BF16)
    grams[0].wait_recv()
    grams[1].wait()
    for copy in sent:
        copy.wait_send()


def on_device(tokens, routes, route_weight, language, lang_weight, w_gate, w_up, w_down):
    langs = jnp.arange(lang_weight.shape[0], dtype=jnp.int32)
    cal = jnp.sum(jnp.where(language[None, :] == langs[:, None], lang_weight[:, None], 0.0), axis=0)
    meta = jnp.concatenate(
        [routes.T.astype(F32), route_weight.T, cal[None, :], jnp.zeros((7, TOK), F32)], axis=0
    )
    rows = CHUNKS * ROWS
    anywhere = pl.BlockSpec(memory_space=pl.ANY)
    return pl.pallas_call(
        kernel,
        out_shape=(
            jax.ShapeDtypeStruct((TOK, DS), BF16),
            jax.ShapeDtypeStruct((2, FS, FF), F32),
        ),
        in_specs=[anywhere] * 5,
        out_specs=(pl.BlockSpec(memory_space=pltpu.VMEM), anywhere),
        scratch_shapes=[
            pltpu.VMEM((NZ * TOK, DS), BF16),
            pltpu.VMEM((NZ, 24, TOK), F32),
            pltpu.VMEM((2, rows, DS), BF16),
            pltpu.VMEM((2, rows, DS), BF16),
            pltpu.VMEM((rows, TOK), BF16),
            pltpu.VMEM((rows, TOK), BF16),
            pltpu.VMEM((rows, D), BF16),
            pltpu.VMEM((2 * FC, D), BF16),
            pltpu.VMEM((2, FF, DS), BF16),
            pltpu.VMEM((rows, FC), BF16),
            pltpu.VMEM((rows, FC), BF16),
            pltpu.VMEM((rows, FF), BF16),
            pltpu.VMEM((2, rows, DS), BF16),
            pltpu.VMEM((2, rows, DS), BF16),
            pltpu.VMEM((CHUNKS, 2 * ROWS, 2 * TOK), BF16),
            pltpu.VMEM((CHUNKS, 2 * ROWS, 2 * TOK), BF16),
            pltpu.VMEM((NZ * TOK, DS), BF16),
            pltpu.VMEM((NZ * TOK, DS), BF16),
            pltpu.VMEM((FC, FF), F32),
            pltpu.SemaphoreType.DMA((NSEM,)),
            pltpu.SemaphoreType.DMA((NSEM,)),
            pltpu.SemaphoreType.DMA((24,)),
        ],
        compiler_params=pltpu.CompilerParams(
            collective_id=0, has_side_effects=True, vmem_limit_bytes=60 * 1024 * 1024
        ),
        name="routed_experts",
    )(tokens, meta, w_gate, w_up, w_down)


def solution(mesh):
    in_specs = (
        P("expert", "col"),
        P("expert", None),
        P("expert", None),
        P("expert"),
        P(),
        P("expert", "col", None),
        P("expert", "col", None),
        P("expert", None, "col"),
    )
    out_specs = (P("expert", "col"), P("expert", "col", None))
    return jax.shard_map(
        on_device, mesh=mesh, in_specs=in_specs, out_specs=out_specs, check_vma=False
    )
```

```python
import jax
import jax.numpy as jnp
from jax import lax
from jax.experimental import pallas as pl
from jax.experimental.pallas import tpu as pltpu
from jax.sharding import PartitionSpec as P

MESH = pl.DeviceIdType.MESH
NZ, NX, NY = 8, 4, 4
TOK = 128
CAP = 24
PAIR = 2 * CAP
ROWS = NX * PAIR
CHUNKS = NZ // 2
HALF = ROWS // 2
ORDER = (0, 2, 3, 1)
D = 4096
DS = 512
FF = 1536
FS = 192
FC = 2 * FS
NSEM = 208

F32 = jnp.float32
BF16 = jnp.bfloat16


def kernel(
    tok_hbm, meta_hbm, wg_hbm, wu_hbm, wd_hbm,
    out_ref, gram_ref,
    tok, meta, pick_send, row_buf, cal_send, cal_buf, xs, w_in, w_dn,
    hid_own, scaled, hid, eo, back, coef_hi, coef_lo, part, part_in, gram,
    send_sem, recv_sem, local_sem,
):
    i = lax.axis_index("expert")
    c = lax.axis_index("col")
    z, x = i // NX, lax.rem(i, NX)
    y, k = c // 2, lax.rem(c, 2)
    other = 1 - k

    def at_z(step):
        return (lax.rem(z + step + NZ, NZ) * NX + x, c)

    def at_x(step, flip=0):
        core = other if flip else k
        return (z * NX + lax.rem(x + step + NX, NX), y * 2 + core)

    def at_y(step, flip=0):
        core = other if flip else k
        return (i, lax.rem(y + step + NY, NY) * 2 + core)

    sibling = (i, y * 2 + other)

    count = [0, 0]
    sent = []

    def remote(src, dst, device):
        n = count[0]
        count[0] += 1
        copy = pltpu.make_async_remote_copy(
            src_ref=src, dst_ref=dst, send_sem=send_sem.at[n], recv_sem=recv_sem.at[n],
            device_id=device, device_id_type=MESH,
        )
        copy.start()
        sent.append(copy)
        return copy

    def local(src, dst):
        n = count[1]
        count[1] += 1
        copy = pltpu.make_async_copy(src, dst, local_sem.at[n])
        copy.start()
        return copy

    def arrive(copies):
        for copy in copies:
            copy.wait_recv()

    own_tok = local(tok_hbm, tok.at[pl.ds(0, TOK), :])
    own_meta = local(meta_hbm, meta.at[0])
    own_rows = pl.ds(pl.multiple_of(k * FS, 64), FS)
    own_rows_up = pl.ds(pl.multiple_of(FC + k * FS, 64), FS)
    weights_local = [
        local(wg_hbm.at[k], w_in.at[own_rows, :]),
        local(wu_hbm.at[k], w_in.at[own_rows_up, :]),
        local(wd_hbm.at[k], w_dn.at[0]),
    ]

    barrier = pltpu.get_barrier_semaphore()
    partners = [at_z(s) for s in range(1, NZ)]
    partners += [at_x(s, f) for s in range(1, NX) for f in range(2)]
    partners += [at_y(s, f) for s in (-1, 1) for f in range(2)]
    partners += [sibling]
    for device in partners:
        pl.semaphore_signal(barrier, inc=1, device_id=device, device_id_type=MESH)
    pl.semaphore_wait(barrier, len(partners))

    def slot_of(offset):
        return 2 * offset if offset >= 0 else 2 * (-offset - 1) + 1

    def z_send(source, target, step):
        a, b = slot_of(source), slot_of(target)
        device = at_z(step)
        return [
            remote(tok.at[pl.ds(a * TOK, TOK), :], tok.at[pl.ds(b * TOK, TOK), :], device),
            remote(meta.at[a], meta.at[b], device),
        ]

    own_tok.wait()
    own_meta.wait()
    right = {1: z_send(0, -1, 1)}
    left = {1: z_send(0, 1, -1)}

    weights_remote = [
        remote(wg_hbm.at[other], w_in.at[own_rows, :], sibling),
        remote(wu_hbm.at[other], w_in.at[own_rows_up, :], sibling),
        remote(wd_hbm.at[other], w_dn.at[1], sibling),
    ]

    lane = lax.broadcasted_iota(jnp.int32, (2 * TOK, 2 * TOK), 1)
    sub = lax.broadcasted_iota(jnp.int32, (2 * TOK, 2 * TOK), 0)
    before = jnp.where((sub < lane) & (sub // TOK == lane // TOK), 1.0, 0.0).astype(BF16)
    block_base = jnp.where(
        lax.broadcasted_iota(jnp.int32, (1, 2 * TOK), 1) >= TOK, float(CAP), 0.0
    )
    row_id = lax.broadcasted_iota(jnp.int32, (PAIR, 2 * TOK), 0).astype(F32)

    picked, cal_in = {}, {}

    def z_forward(hop):
        arrive(right[hop])
        if hop < CHUNKS:
            right[hop + 1] = z_send(-hop, -(hop + 1), 1)
            arrive(left[hop])
        if hop + 1 < CHUNKS:
            left[hop + 1] = z_send(hop, hop + 1, -1)

    def stage_pick(p):
        m0, m1 = meta[2 * p], meta[2 * p + 1]
        pair = jnp.concatenate([m0, m1], axis=1)
        experts, gains = pair[0:8], pair[8:16]
        cal = pair[16:17]
        hits, coefs = [], []
        for flip in range(2):
            for step in range(NX):
                e = (z * NX + lax.rem(x + step, NX)) * 2 + (other if flip else k)
                same = experts == e.astype(F32)
                hits.append(jnp.max(jnp.where(same, 1.0, 0.0), axis=0, keepdims=True))
                coefs.append(jnp.sum(jnp.where(same, gains, 0.0), axis=0, keepdims=True))
        hit = jnp.concatenate(hits, axis=0)
        place = jnp.dot(hit.astype(BF16), before, preferred_element_type=F32)
        where_to = jnp.where(hit > 0.5, place + block_base, -1.0)
        picks = []
        for g in range(2 * NX):
            mask = row_id == where_to[g : g + 1]
            picks.append(jnp.where(mask, 1.0, 0.0).astype(BF16))
            high = coefs[g].astype(BF16).astype(F32)
            coef_hi[p, pl.ds(g * PAIR, PAIR), :] = jnp.where(mask, high, 0.0).astype(BF16)
            coef_lo[p, pl.ds(g * PAIR, PAIR), :] = jnp.where(mask, coefs[g] - high, 0.0).astype(BF16)
            if g < NX:
                col = jnp.sum(jnp.where(mask, cal, 0.0), axis=1, keepdims=True)
                wide = jnp.broadcast_to(col, (PAIR, TOK)).astype(BF16)
                if g == 0:
                    cal_buf[pl.ds(p * ROWS, PAIR), :] = wide
                else:
                    cal_send[pl.ds(p * ROWS + g * PAIR, PAIR), :] = wide
        rows = jnp.dot(
            jnp.concatenate(picks, axis=0), tok[pl.ds(2 * p * TOK, 2 * TOK), :],
            preferred_element_type=F32,
        ).astype(BF16)
        for flip in range(2):
            mine = rows[flip * ROWS : (flip + 1) * ROWS]
            row_buf[flip, pl.ds(p * ROWS, PAIR), :] = mine[0:PAIR]
            pick_send[flip, pl.ds(p * ROWS, ROWS), :] = mine
        picked[p], cal_in[p] = {}, {}
        for step in (3, 1, 2):
            device = at_x(step)
            src = pl.ds(p * ROWS + step * PAIR, PAIR)
            dst = pl.ds(p * ROWS + (NX - step) * PAIR, PAIR)
            picked[p][NX - step] = remote(pick_send.at[:, src, :], row_buf.at[:, dst, :], device)
            cal_in[p][NX - step] = remote(cal_send.at[src, :], cal_buf.at[dst, :], device)

    own_lanes = pl.ds(pl.multiple_of(c * DS, DS), DS)
    own_hid = pl.ds(pl.multiple_of(y * FC, 128), FC)
    left_y, right_y = lax.rem(y + NY - 1, NY), lax.rem(y + 1, NY)
    direct, to_self, forwarded, kept = {}, {}, {}, {}

    def base(n):
        return ORDER[n // 2] * ROWS + n % 2 * HALF

    def slots(n):
        return (2, 3) if n % 2 else (0, 1)

    def stage_spread(n):
        arrive(picked[ORDER[n // 2]][slot] for slot in slots(n) if slot)
        rows = pl.ds(base(n), HALF)
        direct[n] = [
            remote(row_buf.at[flip, rows, :], xs.at[rows, own_lanes], at_y(step, flip))
            for flip in range(2) for step in (1, -1)
        ]
        to_self[n] = remote(row_buf.at[1, rows, :], xs.at[rows, own_lanes], sibling)
        kept[n] = local(row_buf.at[0, rows, :], xs.at[rows, own_lanes])

    def stage_forward(n):
        arrive(direct[n])
        half = HALF // 2
        a = (pl.ds(base(n), half), pl.ds(pl.multiple_of(left_y * 2 * DS, DS), 2 * DS))
        b = (pl.ds(base(n) + half, half), pl.ds(pl.multiple_of(right_y * 2 * DS, DS), 2 * DS))
        forwarded[n] = [
            remote(xs.at[a], xs.at[a], at_y(1)),
            remote(xs.at[b], xs.at[b], at_y(-1)),
        ]

    hid_direct, hid_forwarded, hid_kept = {}, {}, {}

    def stage_hidden(n):
        if n == 0:
            for copy in weights_local[:2]:
                copy.wait()
            arrive(weights_remote[:2])
        arrive(forwarded[n])
        to_self[n].wait_recv()
        kept[n].wait()
        arrive(cal_in[ORDER[n // 2]][slot] for slot in slots(n) if slot)
        rows = pl.ds(base(n), HALF)
        both = lax.dot_general(
            xs[rows, :], w_in[...], (((1,), (1,)), ((), ())), preferred_element_type=F32
        )
        gate, up = both[:, 0:FC], both[:, FC : 2 * FC]
        h = (gate / (1.0 + jnp.exp(-gate)) * up).astype(BF16)
        hid_own[rows, :] = h
        hid_direct[n] = [
            remote(hid_own.at[rows, :], hid.at[rows, own_hid], at_y(step)) for step in (1, -1)
        ]
        hid_kept[n] = local(hid_own.at[rows, :], hid.at[rows, own_hid])
        cal = cal_buf[rows, :][:, 0:1].astype(F32)
        scaled[rows, :] = (cal * h.astype(F32)).astype(BF16)

    def stage_hidden_forward(n):
        arrive(hid_direct[n])
        half = HALF // 2
        a = (pl.ds(base(n), half), pl.ds(pl.multiple_of(left_y * FC, 128), FC))
        b = (pl.ds(base(n) + half, half), pl.ds(pl.multiple_of(right_y * FC, 128), FC))
        hid_forwarded[n] = [
            remote(hid.at[a], hid.at[a], at_y(1)),
            remote(hid.at[b], hid.at[b], at_y(-1)),
        ]

    returned, back_kept = {}, {}

    def stage_down(n):
        p = ORDER[n // 2]
        if n == 0:
            weights_local[2].wait()
            arrive(weights_remote[2:])
        arrive(hid_forwarded[n])
        hid_kept[n].wait()
        rows = pl.ds(base(n), HALF)
        for flip in range(2):
            eo[flip, rows, :] = jnp.dot(
                hid[rows, :], w_dn[flip], preferred_element_type=F32
            ).astype(BF16)
        returned.setdefault(p, [])
        for step in slots(n):
            src = pl.ds(p * ROWS + step * PAIR, PAIR)
            dst = pl.ds(p * ROWS + (NX - step) % NX * PAIR, PAIR)
            for flip in range(2):
                if step == 0 and flip == 0:
                    back_kept[p] = local(eo.at[0, src, :], back.at[0, dst, :])
                else:
                    returned[p].append(
                        remote(eo.at[flip, src, :], back.at[flip, dst, :], at_x(step, flip))
                    )

    parts = []

    def stage_combine(p):
        arrive(returned[p])
        back_kept[p].wait()
        rows = back[:, pl.ds(p * ROWS, ROWS), :].reshape(2 * ROWS, DS)
        dims = (((0,), (0,)), ((), ()))
        total = lax.dot_general(coef_hi[p], rows, dims, preferred_element_type=F32)
        total = total + lax.dot_general(coef_lo[p], rows, dims, preferred_element_type=F32)
        part[pl.ds(2 * p * TOK, 2 * TOK), :] = total.astype(BF16)
        for b in range(2):
            if p == 0 and b == 0:
                continue
            s = pl.ds((2 * p + b) * TOK, TOK)
            offset = p if b == 0 else -(p + 1)
            parts.append((s, remote(part.at[s, :], part_in.at[s, :], at_z(offset))))

    grams = []

    def stage_gram():
        gram[...] = lax.dot_general(
            scaled[...], hid[...], (((0,), (0,)), ((), ())), preferred_element_type=F32
        )
        mine = pl.ds(pl.multiple_of(k * FS, 64), FS)
        theirs = pl.ds(pl.multiple_of(other * FS, 64), FS)
        grams.append(remote(gram.at[theirs, :], gram_ref.at[k], sibling))
        grams.append(local(gram.at[mine, :], gram_ref.at[k]))

    halves = 2 * CHUNKS
    z_forward(1)
    stage_pick(0)
    z_forward(2)
    for n in range(halves + 5):
        if n < halves:
            stage_spread(n)
        if n == 1:
            z_forward(3)
            stage_pick(ORDER[1])
        if 1 <= n <= halves:
            stage_forward(n - 1)
        if n == 1:
            z_forward(4)
        if n in (2, 4):
            stage_pick(ORDER[n // 2 + 1])
        if 2 <= n < halves + 2:
            stage_hidden(n - 2)
        if 3 <= n < halves + 3:
            stage_hidden_forward(n - 3)
        if 4 <= n < halves + 4:
            stage_down(n - 4)
        if n == halves + 4:
            stage_gram()
        if n >= 6 and n % 2 == 0:
            stage_combine(ORDER[n // 2 - 3])

    total = part[pl.ds(0, TOK), :].astype(F32)
    for s, copy in parts:
        copy.wait_recv()
        total = total + part_in[s, :].astype(F32)
    out_ref[...] = total.astype(BF16)
    grams[0].wait_recv()
    grams[1].wait()
    for copy in sent:
        copy.wait_send()


def on_device(tokens, routes, route_weight, language, lang_weight, w_gate, w_up, w_down):
    langs = jnp.arange(lang_weight.shape[0], dtype=jnp.int32)
    cal = jnp.sum(jnp.where(language[None, :] == langs[:, None], lang_weight[:, None], 0.0), axis=0)
    meta = jnp.concatenate(
        [routes.T.astype(F32), route_weight.T, cal[None, :], jnp.zeros((7, TOK), F32)], axis=0
    )
    rows = CHUNKS * ROWS
    anywhere = pl.BlockSpec(memory_space=pl.ANY)
    return pl.pallas_call(
        kernel,
        out_shape=(
            jax.ShapeDtypeStruct((TOK, DS), BF16),
            jax.ShapeDtypeStruct((2, FS, FF), F32),
        ),
        in_specs=[anywhere] * 5,
        out_specs=(pl.BlockSpec(memory_space=pltpu.VMEM), anywhere),
        scratch_shapes=[
            pltpu.VMEM((NZ * TOK, DS), BF16),
            pltpu.VMEM((NZ, 24, TOK), F32),
            pltpu.VMEM((2, rows, DS), BF16),
            pltpu.VMEM((2, rows, DS), BF16),
            pltpu.VMEM((rows, TOK), BF16),
            pltpu.VMEM((rows, TOK), BF16),
            pltpu.VMEM((rows, D), BF16),
            pltpu.VMEM((2 * FC, D), BF16),
            pltpu.VMEM((2, FF, DS), BF16),
            pltpu.VMEM((rows, FC), BF16),
            pltpu.VMEM((rows, FC), BF16),
            pltpu.VMEM((rows, FF), BF16),
            pltpu.VMEM((2, rows, DS), BF16),
            pltpu.VMEM((2, rows, DS), BF16),
            pltpu.VMEM((CHUNKS, 2 * ROWS, 2 * TOK), BF16),
            pltpu.VMEM((CHUNKS, 2 * ROWS, 2 * TOK), BF16),
            pltpu.VMEM((NZ * TOK, DS), BF16),
            pltpu.VMEM((NZ * TOK, DS), BF16),
            pltpu.VMEM((FC, FF), F32),
            pltpu.SemaphoreType.DMA((NSEM,)),
            pltpu.SemaphoreType.DMA((NSEM,)),
            pltpu.SemaphoreType.DMA((40,)),
        ],
        compiler_params=pltpu.CompilerParams(
            collective_id=0, has_side_effects=True, vmem_limit_bytes=60 * 1024 * 1024
        ),
        name="routed_experts",
    )(tokens, meta, w_gate, w_up, w_down)


def solution(mesh):
    in_specs = (
        P("expert", "col"),
        P("expert", None),
        P("expert", None),
        P("expert"),
        P(),
        P("expert", "col", None),
        P("expert", "col", None),
        P("expert", None, "col"),
    )
    out_specs = (P("expert", "col"), P("expert", "col", None))
    return jax.shard_map(
        on_device, mesh=mesh, in_specs=in_specs, out_specs=out_specs, check_vma=False
    )
```

```python
import jax
import jax.numpy as jnp
from jax import lax
from jax.experimental import pallas as pl
from jax.experimental.pallas import tpu as pltpu
from jax.sharding import PartitionSpec as P

MESH = pl.DeviceIdType.MESH
NZ, NX, NY = 8, 4, 4
TOK = 128
CAP = 24
PAIR = 2 * CAP
ROWS = NX * PAIR
CHUNKS = NZ // 2
HALF = ROWS // 2
ORDER = (0, 3, 2, 1)
D = 4096
DS = 512
FF = 1536
FS = 192
FC = 2 * FS
NSEM = 208

F32 = jnp.float32
BF16 = jnp.bfloat16


def kernel(
    tok_hbm, meta_hbm, wg_hbm, wu_hbm, wd_hbm,
    out_ref, gram_ref,
    tok, meta, pick_send, row_buf, cal_send, cal_buf, xs, w_in, w_dn,
    hid_own, scaled, hid, eo, back, coef_hi, coef_lo, part, part_in, gram,
    send_sem, recv_sem, local_sem,
):
    i = lax.axis_index("expert")
    c = lax.axis_index("col")
    z, x = i // NX, lax.rem(i, NX)
    y, k = c // 2, lax.rem(c, 2)
    other = 1 - k

    def at_z(step):
        return (lax.rem(z + step + NZ, NZ) * NX + x, c)

    def at_x(step, flip=0):
        core = other if flip else k
        return (z * NX + lax.rem(x + step + NX, NX), y * 2 + core)

    def at_y(step, flip=0):
        core = other if flip else k
        return (i, lax.rem(y + step + NY, NY) * 2 + core)

    sibling = (i, y * 2 + other)

    count = [0, 0]
    sent = []

    def remote(src, dst, device):
        n = count[0]
        count[0] += 1
        copy = pltpu.make_async_remote_copy(
            src_ref=src, dst_ref=dst, send_sem=send_sem.at[n], recv_sem=recv_sem.at[n],
            device_id=device, device_id_type=MESH,
        )
        copy.start()
        sent.append(copy)
        return copy

    def local(src, dst):
        n = count[1]
        count[1] += 1
        copy = pltpu.make_async_copy(src, dst, local_sem.at[n])
        copy.start()
        return copy

    def arrive(copies):
        for copy in copies:
            copy.wait_recv()

    own_tok = local(tok_hbm, tok.at[pl.ds(0, TOK), :])
    own_meta = local(meta_hbm, meta.at[0])
    own_rows = pl.ds(pl.multiple_of(k * FS, 64), FS)
    own_rows_up = pl.ds(pl.multiple_of(FC + k * FS, 64), FS)
    weights_local = [
        local(wg_hbm.at[k], w_in.at[own_rows, :]),
        local(wu_hbm.at[k], w_in.at[own_rows_up, :]),
        local(wd_hbm.at[k], w_dn.at[0]),
    ]

    barrier = pltpu.get_barrier_semaphore()
    partners = [at_z(s) for s in range(1, NZ)]
    partners += [at_x(s, f) for s in range(1, NX) for f in range(2)]
    partners += [at_y(s, f) for s in (-1, 1) for f in range(2)]
    partners += [sibling]
    for device in partners:
        pl.semaphore_signal(barrier, inc=1, device_id=device, device_id_type=MESH)
    pl.semaphore_wait(barrier, len(partners))

    def slot_of(offset):
        return 2 * offset if offset >= 0 else 2 * (-offset - 1) + 1

    def z_send(source, target, step):
        a, b = slot_of(source), slot_of(target)
        device = at_z(step)
        return [
            remote(tok.at[pl.ds(a * TOK, TOK), :], tok.at[pl.ds(b * TOK, TOK), :], device),
            remote(meta.at[a], meta.at[b], device),
        ]

    own_tok.wait()
    own_meta.wait()
    right = {1: z_send(0, -1, 1)}
    left = {1: z_send(0, 1, -1)}

    weights_remote = [
        remote(wg_hbm.at[other], w_in.at[own_rows, :], sibling),
        remote(wu_hbm.at[other], w_in.at[own_rows_up, :], sibling),
        remote(wd_hbm.at[other], w_dn.at[1], sibling),
    ]

    lane = lax.broadcasted_iota(jnp.int32, (2 * TOK, 2 * TOK), 1)
    sub = lax.broadcasted_iota(jnp.int32, (2 * TOK, 2 * TOK), 0)
    before = jnp.where((sub < lane) & (sub // TOK == lane // TOK), 1.0, 0.0).astype(BF16)
    block_base = jnp.where(
        lax.broadcasted_iota(jnp.int32, (1, 2 * TOK), 1) >= TOK, float(CAP), 0.0
    )
    row_id = lax.broadcasted_iota(jnp.int32, (PAIR, 2 * TOK), 0).astype(F32)

    picked, cal_in = {}, {}

    def z_forward(hop):
        arrive(right[hop])
        if hop < CHUNKS:
            right[hop + 1] = z_send(-hop, -(hop + 1), 1)
            arrive(left[hop])
        if hop + 1 < CHUNKS:
            left[hop + 1] = z_send(hop, hop + 1, -1)

    def stage_pick(p):
        m0, m1 = meta[2 * p], meta[2 * p + 1]
        pair = jnp.concatenate([m0, m1], axis=1)
        experts, gains = pair[0:8], pair[8:16]
        cal = pair[16:17]
        hits, coefs = [], []
        for flip in range(2):
            for step in range(NX):
                e = (z * NX + lax.rem(x + step, NX)) * 2 + (other if flip else k)
                same = experts == e.astype(F32)
                hits.append(jnp.max(jnp.where(same, 1.0, 0.0), axis=0, keepdims=True))
                coefs.append(jnp.sum(jnp.where(same, gains, 0.0), axis=0, keepdims=True))
        hit = jnp.concatenate(hits, axis=0)
        place = jnp.dot(hit.astype(BF16), before, preferred_element_type=F32)
        where_to = jnp.where(hit > 0.5, place + block_base, -1.0)
        picks = []
        for g in range(2 * NX):
            mask = row_id == where_to[g : g + 1]
            picks.append(jnp.where(mask, 1.0, 0.0).astype(BF16))
            high = coefs[g].astype(BF16).astype(F32)
            coef_hi[p, pl.ds(g * PAIR, PAIR), :] = jnp.where(mask, high, 0.0).astype(BF16)
            coef_lo[p, pl.ds(g * PAIR, PAIR), :] = jnp.where(mask, coefs[g] - high, 0.0).astype(BF16)
            if g < NX:
                col = jnp.sum(jnp.where(mask, cal, 0.0), axis=1, keepdims=True)
                wide = jnp.broadcast_to(col, (PAIR, TOK)).astype(BF16)
                if g == 0:
                    cal_buf[pl.ds(p * ROWS, PAIR), :] = wide
                else:
                    cal_send[pl.ds(p * ROWS + g * PAIR, PAIR), :] = wide
        rows = jnp.dot(
            jnp.concatenate(picks, axis=0), tok[pl.ds(2 * p * TOK, 2 * TOK), :],
            preferred_element_type=F32,
        ).astype(BF16)
        for flip in range(2):
            mine = rows[flip * ROWS : (flip + 1) * ROWS]
            row_buf[flip, pl.ds(p * ROWS, PAIR), :] = mine[0:PAIR]
            pick_send[flip, pl.ds(p * ROWS, ROWS), :] = mine
        picked[p], cal_in[p] = {}, {}
        for step in (3, 1, 2):
            device = at_x(step)
            src = pl.ds(p * ROWS + step * PAIR, PAIR)
            dst = pl.ds(p * ROWS + (NX - step) * PAIR, PAIR)
            picked[p][NX - step] = remote(pick_send.at[:, src, :], row_buf.at[:, dst, :], device)
            cal_in[p][NX - step] = remote(cal_send.at[src, :], cal_buf.at[dst, :], device)

    own_lanes = pl.ds(pl.multiple_of(c * DS, DS), DS)
    own_hid = pl.ds(pl.multiple_of(y * FC, 128), FC)
    left_y, right_y = lax.rem(y + NY - 1, NY), lax.rem(y + 1, NY)
    direct, to_self, forwarded, kept = {}, {}, {}, {}

    def second(n):
        return 1 - n % 2 if n // 2 == CHUNKS - 1 else n % 2

    def base(n):
        return ORDER[n // 2] * ROWS + second(n) * HALF

    def slots(n):
        return (2, 3) if second(n) else (0, 1)

    def stage_spread(n):
        arrive(picked[ORDER[n // 2]][slot] for slot in slots(n) if slot)
        rows = pl.ds(base(n), HALF)
        direct[n] = [
            remote(row_buf.at[flip, rows, :], xs.at[rows, own_lanes], at_y(step, flip))
            for flip in range(2) for step in (1, -1)
        ]
        to_self[n] = remote(row_buf.at[1, rows, :], xs.at[rows, own_lanes], sibling)
        kept[n] = local(row_buf.at[0, rows, :], xs.at[rows, own_lanes])

    def stage_forward(n):
        arrive(direct[n])
        half = HALF // 2
        a = (pl.ds(base(n), half), pl.ds(pl.multiple_of(left_y * 2 * DS, DS), 2 * DS))
        b = (pl.ds(base(n) + half, half), pl.ds(pl.multiple_of(right_y * 2 * DS, DS), 2 * DS))
        forwarded[n] = [
            remote(xs.at[a], xs.at[a], at_y(1)),
            remote(xs.at[b], xs.at[b], at_y(-1)),
        ]

    hid_direct, hid_forwarded, hid_kept = {}, {}, {}

    def stage_hidden(n):
        if n == 0:
            for copy in weights_local[:2]:
                copy.wait()
            arrive(weights_remote[:2])
        arrive(forwarded[n])
        to_self[n].wait_recv()
        kept[n].wait()
        arrive(cal_in[ORDER[n // 2]][slot] for slot in slots(n) if slot)
        rows = pl.ds(base(n), HALF)
        both = lax.dot_general(
            xs[rows, :], w_in[...], (((1,), (1,)), ((), ())), preferred_element_type=F32
        )
        gate, up = both[:, 0:FC], both[:, FC : 2 * FC]
        h = (gate / (1.0 + jnp.exp(-gate)) * up).astype(BF16)
        hid_own[rows, :] = h
        hid_direct[n] = [
            remote(hid_own.at[rows, :], hid.at[rows, own_hid], at_y(step)) for step in (1, -1)
        ]
        hid_kept[n] = local(hid_own.at[rows, :], hid.at[rows, own_hid])
        cal = cal_buf[rows, :][:, 0:1].astype(F32)
        scaled[rows, :] = (cal * h.astype(F32)).astype(BF16)

    def stage_hidden_forward(n):
        arrive(hid_direct[n])
        half = HALF // 2
        a = (pl.ds(base(n), half), pl.ds(pl.multiple_of(left_y * FC, 128), FC))
        b = (pl.ds(base(n) + half, half), pl.ds(pl.multiple_of(right_y * FC, 128), FC))
        hid_forwarded[n] = [
            remote(hid.at[a], hid.at[a], at_y(1)),
            remote(hid.at[b], hid.at[b], at_y(-1)),
        ]

    returned, back_kept = {}, {}

    def stage_down(n):
        p = ORDER[n // 2]
        if n == 0:
            weights_local[2].wait()
            arrive(weights_remote[2:])
        arrive(hid_forwarded[n])
        hid_kept[n].wait()
        rows = pl.ds(base(n), HALF)
        for flip in range(2):
            eo[flip, rows, :] = jnp.dot(
                hid[rows, :], w_dn[flip], preferred_element_type=F32
            ).astype(BF16)
        returned.setdefault(p, [])
        for step in slots(n):
            src = pl.ds(p * ROWS + step * PAIR, PAIR)
            dst = pl.ds(p * ROWS + (NX - step) % NX * PAIR, PAIR)
            for flip in range(2):
                if step == 0 and flip == 0:
                    back_kept[p] = local(eo.at[0, src, :], back.at[0, dst, :])
                else:
                    returned[p].append(
                        remote(eo.at[flip, src, :], back.at[flip, dst, :], at_x(step, flip))
                    )

    parts = []

    def stage_combine(p):
        arrive(returned[p])
        back_kept[p].wait()
        rows = back[:, pl.ds(p * ROWS, ROWS), :].reshape(2 * ROWS, DS)
        dims = (((0,), (0,)), ((), ()))
        for blocks in ((1,), (0,)) if p == ORDER[-1] else ((0, 1),):
            lanes = slice(blocks[0] * TOK, (blocks[-1] + 1) * TOK)
            total = lax.dot_general(
                coef_hi[p, :, lanes], rows, dims, preferred_element_type=F32
            )
            total = total + lax.dot_general(
                coef_lo[p, :, lanes], rows, dims, preferred_element_type=F32
            )
            into = pl.ds((2 * p + blocks[0]) * TOK, len(blocks) * TOK)
            part[into, :] = total.astype(BF16)
            for b in blocks:
                if p == 0 and b == 0:
                    continue
                s = pl.ds((2 * p + b) * TOK, TOK)
                offset = p if b == 0 else -(p + 1)
                parts.append((s, remote(part.at[s, :], part_in.at[s, :], at_z(offset))))

    grams = []

    def stage_gram():
        gram[...] = lax.dot_general(
            scaled[...], hid[...], (((0,), (0,)), ((), ())), preferred_element_type=F32
        )
        mine = pl.ds(pl.multiple_of(k * FS, 64), FS)
        theirs = pl.ds(pl.multiple_of(other * FS, 64), FS)
        grams.append(remote(gram.at[theirs, :], gram_ref.at[k], sibling))
        grams.append(local(gram.at[mine, :], gram_ref.at[k]))

    halves = 2 * CHUNKS
    z_forward(1)
    stage_pick(0)
    z_forward(2)
    for n in range(halves + 5):
        if n < halves and n != 2:
            stage_spread(n)
        if n == 1:
            z_forward(3)
        if 1 <= n <= halves:
            stage_forward(n - 1)
        if n == 1:
            z_forward(4)
            stage_pick(ORDER[1])
        if n == 2:
            stage_pick(ORDER[2])
            stage_spread(n)
        if n == 4:
            stage_pick(ORDER[3])
        if 2 <= n < halves + 2:
            stage_hidden(n - 2)
        if 3 <= n < halves + 3:
            stage_hidden_forward(n - 3)
        if 4 <= n < halves + 4:
            stage_down(n - 4)
        if n == halves + 4:
            stage_gram()
        if n >= 6 and n % 2 == 0:
            stage_combine(ORDER[n // 2 - 3])

    total = part[pl.ds(0, TOK), :].astype(F32)
    for s, copy in parts:
        copy.wait_recv()
        total = total + part_in[s, :].astype(F32)
    out_ref[...] = total.astype(BF16)
    grams[0].wait_recv()
    grams[1].wait()
    for copy in sent:
        copy.wait_send()


def on_device(tokens, routes, route_weight, language, lang_weight, w_gate, w_up, w_down):
    langs = jnp.arange(lang_weight.shape[0], dtype=jnp.int32)
    cal = jnp.sum(jnp.where(language[None, :] == langs[:, None], lang_weight[:, None], 0.0), axis=0)
    meta = jnp.concatenate(
        [routes.T.astype(F32), route_weight.T, cal[None, :], jnp.zeros((7, TOK), F32)], axis=0
    )
    rows = CHUNKS * ROWS
    anywhere = pl.BlockSpec(memory_space=pl.ANY)
    return pl.pallas_call(
        kernel,
        out_shape=(
            jax.ShapeDtypeStruct((TOK, DS), BF16),
            jax.ShapeDtypeStruct((2, FS, FF), F32),
        ),
        in_specs=[anywhere] * 5,
        out_specs=(pl.BlockSpec(memory_space=pltpu.VMEM), anywhere),
        scratch_shapes=[
            pltpu.VMEM((NZ * TOK, DS), BF16),
            pltpu.VMEM((NZ, 24, TOK), F32),
            pltpu.VMEM((2, rows, DS), BF16),
            pltpu.VMEM((2, rows, DS), BF16),
            pltpu.VMEM((rows, TOK), BF16),
            pltpu.VMEM((rows, TOK), BF16),
            pltpu.VMEM((rows, D), BF16),
            pltpu.VMEM((2 * FC, D), BF16),
            pltpu.VMEM((2, FF, DS), BF16),
            pltpu.VMEM((rows, FC), BF16),
            pltpu.VMEM((rows, FC), BF16),
            pltpu.VMEM((rows, FF), BF16),
            pltpu.VMEM((2, rows, DS), BF16),
            pltpu.VMEM((2, rows, DS), BF16),
            pltpu.VMEM((CHUNKS, 2 * ROWS, 2 * TOK), BF16),
            pltpu.VMEM((CHUNKS, 2 * ROWS, 2 * TOK), BF16),
            pltpu.VMEM((NZ * TOK, DS), BF16),
            pltpu.VMEM((NZ * TOK, DS), BF16),
            pltpu.VMEM((FC, FF), F32),
            pltpu.SemaphoreType.DMA((NSEM,)),
            pltpu.SemaphoreType.DMA((NSEM,)),
            pltpu.SemaphoreType.DMA((40,)),
        ],
        compiler_params=pltpu.CompilerParams(
            collective_id=0, has_side_effects=True, vmem_limit_bytes=60 * 1024 * 1024
        ),
        name="routed_experts",
    )(tokens, meta, w_gate, w_up, w_down)


def solution(mesh):
    in_specs = (
        P("expert", "col"),
        P("expert", None),
        P("expert", None),
        P("expert"),
        P(),
        P("expert", "col", None),
        P("expert", "col", None),
        P("expert", None, "col"),
    )
    out_specs = (P("expert", "col"), P("expert", "col", None))
    return jax.shard_map(
        on_device, mesh=mesh, in_specs=in_specs, out_specs=out_specs, check_vma=False
    )
```

```python
import jax
import jax.numpy as jnp
from jax import lax
from jax.experimental import pallas as pl
from jax.experimental.pallas import tpu as pltpu
from jax.sharding import PartitionSpec as P

MESH = pl.DeviceIdType.MESH
NZ, NX, NY = 8, 4, 4
TOK = 128
CAP = 24
PAIR = 2 * CAP
ROWS = NX * PAIR
CHUNKS = NZ // 2
HALF = ROWS // 2
ORDER = (0, 3, 2, 1)
D = 4096
DS = 512
FF = 1536
FS = 192
FC = 2 * FS
NSEM = 208

F32 = jnp.float32
BF16 = jnp.bfloat16


def kernel(
    tok_hbm, routes_hbm, gains_hbm, cal_hbm, wg_hbm, wu_hbm, wd_hbm,
    out_ref, gram_ref,
    tok, routes, gains, cals, meta, pick_send, row_buf, cal_send, cal_buf, xs, w_in, w_dn,
    hid_own, scaled, hid, eo, back, coef_hi, coef_lo, part, part_in, gram,
    send_sem, recv_sem, local_sem,
):
    i = lax.axis_index("expert")
    c = lax.axis_index("col")
    z, x = i // NX, lax.rem(i, NX)
    y, k = c // 2, lax.rem(c, 2)
    other = 1 - k

    def at_z(step):
        return (lax.rem(z + step + NZ, NZ) * NX + x, c)

    def at_x(step, flip=0):
        core = other if flip else k
        return (z * NX + lax.rem(x + step + NX, NX), y * 2 + core)

    def at_y(step, flip=0):
        core = other if flip else k
        return (i, lax.rem(y + step + NY, NY) * 2 + core)

    sibling = (i, y * 2 + other)

    count = [0, 0]
    sent = []

    def remote(src, dst, device):
        n = count[0]
        count[0] += 1
        copy = pltpu.make_async_remote_copy(
            src_ref=src, dst_ref=dst, send_sem=send_sem.at[n], recv_sem=recv_sem.at[n],
            device_id=device, device_id_type=MESH,
        )
        copy.start()
        sent.append(copy)
        return copy

    def local(src, dst):
        n = count[1]
        count[1] += 1
        copy = pltpu.make_async_copy(src, dst, local_sem.at[n])
        copy.start()
        return copy

    def arrive(copies):
        for copy in copies:
            copy.wait_recv()

    own_tok = local(tok_hbm, tok.at[pl.ds(0, TOK), :])
    own_meta = [local(routes_hbm, routes), local(gains_hbm, gains), local(cal_hbm, cals)]
    own_rows = pl.ds(pl.multiple_of(k * FS, 64), FS)
    own_rows_up = pl.ds(pl.multiple_of(FC + k * FS, 64), FS)
    weights_local = [
        local(wg_hbm.at[k], w_in.at[own_rows, :]),
        local(wu_hbm.at[k], w_in.at[own_rows_up, :]),
        local(wd_hbm.at[k], w_dn.at[0]),
    ]

    barrier = pltpu.get_barrier_semaphore()
    partners = [at_z(s) for s in range(1, NZ)]
    partners += [at_x(s, f) for s in range(1, NX) for f in range(2)]
    partners += [at_y(s, f) for s in (-1, 1) for f in range(2)]
    partners += [sibling]
    for device in partners:
        pl.semaphore_signal(barrier, inc=1, device_id=device, device_id_type=MESH)
    for copy in own_meta:
        copy.wait()
    meta[0] = jnp.concatenate(
        [routes[...].astype(F32), gains[...], jnp.broadcast_to(cals[...], (8, TOK))], axis=0
    )
    pl.semaphore_wait(barrier, len(partners))

    def slot_of(offset):
        return 2 * offset if offset >= 0 else 2 * (-offset - 1) + 1

    def z_send(source, target, step):
        a, b = slot_of(source), slot_of(target)
        device = at_z(step)
        return [
            remote(tok.at[pl.ds(a * TOK, TOK), :], tok.at[pl.ds(b * TOK, TOK), :], device),
            remote(meta.at[a], meta.at[b], device),
        ]

    own_tok.wait()
    right = {1: z_send(0, -1, 1)}
    left = {1: z_send(0, 1, -1)}

    weights_remote = [
        remote(wg_hbm.at[other], w_in.at[own_rows, :], sibling),
        remote(wu_hbm.at[other], w_in.at[own_rows_up, :], sibling),
        remote(wd_hbm.at[other], w_dn.at[1], sibling),
    ]

    lane = lax.broadcasted_iota(jnp.int32, (2 * TOK, 2 * TOK), 1)
    sub = lax.broadcasted_iota(jnp.int32, (2 * TOK, 2 * TOK), 0)
    before = jnp.where((sub < lane) & (sub // TOK == lane // TOK), 1.0, 0.0).astype(BF16)
    block_base = jnp.where(
        lax.broadcasted_iota(jnp.int32, (1, 2 * TOK), 1) >= TOK, float(CAP), 0.0
    )
    row_id = lax.broadcasted_iota(jnp.int32, (PAIR, 2 * TOK), 0).astype(F32)

    picked, cal_in = {}, {}

    def z_forward(hop):
        arrive(right[hop])
        if hop < CHUNKS:
            right[hop + 1] = z_send(-hop, -(hop + 1), 1)
            arrive(left[hop])
        if hop + 1 < CHUNKS:
            left[hop + 1] = z_send(hop, hop + 1, -1)

    def stage_pick(p):
        m0, m1 = meta[2 * p], meta[2 * p + 1]
        pair = jnp.concatenate([m0, m1], axis=1)
        experts, gains = pair[0:8], pair[8:16]
        cal = pair[16:17]
        hits, coefs = [], []
        for flip in range(2):
            for step in range(NX):
                e = (z * NX + lax.rem(x + step, NX)) * 2 + (other if flip else k)
                same = experts == e.astype(F32)
                hits.append(jnp.max(jnp.where(same, 1.0, 0.0), axis=0, keepdims=True))
                coefs.append(jnp.sum(jnp.where(same, gains, 0.0), axis=0, keepdims=True))
        hit = jnp.concatenate(hits, axis=0)
        place = jnp.dot(hit.astype(BF16), before, preferred_element_type=F32)
        where_to = jnp.where(hit > 0.5, place + block_base, -1.0)
        picks = []
        for g in range(2 * NX):
            mask = row_id == where_to[g : g + 1]
            picks.append(jnp.where(mask, 1.0, 0.0).astype(BF16))
            high = coefs[g].astype(BF16).astype(F32)
            coef_hi[p, pl.ds(g * PAIR, PAIR), :] = jnp.where(mask, high, 0.0).astype(BF16)
            coef_lo[p, pl.ds(g * PAIR, PAIR), :] = jnp.where(mask, coefs[g] - high, 0.0).astype(BF16)
            if g < NX:
                col = jnp.sum(jnp.where(mask, cal, 0.0), axis=1, keepdims=True)
                wide = jnp.broadcast_to(col, (PAIR, TOK)).astype(BF16)
                if g == 0:
                    cal_buf[pl.ds(p * ROWS, PAIR), :] = wide
                else:
                    cal_send[pl.ds(p * ROWS + g * PAIR, PAIR), :] = wide
        rows = jnp.dot(
            jnp.concatenate(picks, axis=0), tok[pl.ds(2 * p * TOK, 2 * TOK), :],
            preferred_element_type=F32,
        ).astype(BF16)
        for flip in range(2):
            mine = rows[flip * ROWS : (flip + 1) * ROWS]
            row_buf[flip, pl.ds(p * ROWS, PAIR), :] = mine[0:PAIR]
            pick_send[flip, pl.ds(p * ROWS, ROWS), :] = mine
        picked[p], cal_in[p] = {}, {}
        for step in (3, 1, 2):
            device = at_x(step)
            src = pl.ds(p * ROWS + step * PAIR, PAIR)
            dst = pl.ds(p * ROWS + (NX - step) * PAIR, PAIR)
            picked[p][NX - step] = remote(pick_send.at[:, src, :], row_buf.at[:, dst, :], device)
            cal_in[p][NX - step] = remote(cal_send.at[src, :], cal_buf.at[dst, :], device)

    own_lanes = pl.ds(pl.multiple_of(c * DS, DS), DS)
    own_hid = pl.ds(pl.multiple_of(y * FC, 128), FC)
    left_y, right_y = lax.rem(y + NY - 1, NY), lax.rem(y + 1, NY)
    direct, to_self, forwarded, kept = {}, {}, {}, {}

    def second(n):
        return 1 - n % 2 if n // 2 == CHUNKS - 1 else n % 2

    def base(n):
        return ORDER[n // 2] * ROWS + second(n) * HALF

    def slots(n):
        return (2, 3) if second(n) else (0, 1)

    def stage_spread(n):
        arrive(picked[ORDER[n // 2]][slot] for slot in slots(n) if slot)
        rows = pl.ds(base(n), HALF)
        direct[n] = [
            remote(row_buf.at[flip, rows, :], xs.at[rows, own_lanes], at_y(step, flip))
            for flip in range(2) for step in (1, -1)
        ]
        to_self[n] = remote(row_buf.at[1, rows, :], xs.at[rows, own_lanes], sibling)
        kept[n] = local(row_buf.at[0, rows, :], xs.at[rows, own_lanes])

    def stage_forward(n):
        arrive(direct[n])
        half = HALF // 2
        a = (pl.ds(base(n), half), pl.ds(pl.multiple_of(left_y * 2 * DS, DS), 2 * DS))
        b = (pl.ds(base(n) + half, half), pl.ds(pl.multiple_of(right_y * 2 * DS, DS), 2 * DS))
        forwarded[n] = [
            remote(xs.at[a], xs.at[a], at_y(1)),
            remote(xs.at[b], xs.at[b], at_y(-1)),
        ]

    hid_direct, hid_forwarded, hid_kept = {}, {}, {}

    def stage_hidden(n):
        if n == 0:
            for copy in weights_local[:2]:
                copy.wait()
            arrive(weights_remote[:2])
        arrive(forwarded[n])
        to_self[n].wait_recv()
        kept[n].wait()
        arrive(cal_in[ORDER[n // 2]][slot] for slot in slots(n) if slot)
        rows = pl.ds(base(n), HALF)
        both = lax.dot_general(
            xs[rows, :], w_in[...], (((1,), (1,)), ((), ())), preferred_element_type=F32
        )
        gate, up = both[:, 0:FC], both[:, FC : 2 * FC]
        h = (gate / (1.0 + jnp.exp(-gate)) * up).astype(BF16)
        hid_own[rows, :] = h
        hid_direct[n] = [
            remote(hid_own.at[rows, :], hid.at[rows, own_hid], at_y(step)) for step in (1, -1)
        ]
        hid_kept[n] = local(hid_own.at[rows, :], hid.at[rows, own_hid])
        cal = cal_buf[rows, :][:, 0:1].astype(F32)
        scaled[rows, :] = (cal * h.astype(F32)).astype(BF16)

    def stage_hidden_forward(n):
        arrive(hid_direct[n])
        half = HALF // 2
        a = (pl.ds(base(n), half), pl.ds(pl.multiple_of(left_y * FC, 128), FC))
        b = (pl.ds(base(n) + half, half), pl.ds(pl.multiple_of(right_y * FC, 128), FC))
        hid_forwarded[n] = [
            remote(hid.at[a], hid.at[a], at_y(1)),
            remote(hid.at[b], hid.at[b], at_y(-1)),
        ]

    returned, back_kept = {}, {}

    def stage_down(n):
        p = ORDER[n // 2]
        if n == 0:
            weights_local[2].wait()
            arrive(weights_remote[2:])
        arrive(hid_forwarded[n])
        hid_kept[n].wait()
        rows = pl.ds(base(n), HALF)
        for flip in range(2):
            eo[flip, rows, :] = jnp.dot(
                hid[rows, :], w_dn[flip], preferred_element_type=F32
            ).astype(BF16)
        returned.setdefault(p, [])
        for step in slots(n):
            src = pl.ds(p * ROWS + step * PAIR, PAIR)
            dst = pl.ds(p * ROWS + (NX - step) % NX * PAIR, PAIR)
            for flip in range(2):
                if step == 0 and flip == 0:
                    back_kept[p] = local(eo.at[0, src, :], back.at[0, dst, :])
                else:
                    returned[p].append(
                        remote(eo.at[flip, src, :], back.at[flip, dst, :], at_x(step, flip))
                    )

    parts = []

    def stage_combine(p):
        arrive(returned[p])
        back_kept[p].wait()
        rows = back[:, pl.ds(p * ROWS, ROWS), :].reshape(2 * ROWS, DS)
        dims = (((0,), (0,)), ((), ()))
        for blocks in ((1,), (0,)) if p == ORDER[-1] else ((0, 1),):
            lanes = slice(blocks[0] * TOK, (blocks[-1] + 1) * TOK)
            total = lax.dot_general(
                coef_hi[p, :, lanes], rows, dims, preferred_element_type=F32
            )
            total = total + lax.dot_general(
                coef_lo[p, :, lanes], rows, dims, preferred_element_type=F32
            )
            into = pl.ds((2 * p + blocks[0]) * TOK, len(blocks) * TOK)
            part[into, :] = total.astype(BF16)
            for b in blocks:
                if p == 0 and b == 0:
                    continue
                s = pl.ds((2 * p + b) * TOK, TOK)
                offset = p if b == 0 else -(p + 1)
                parts.append((s, remote(part.at[s, :], part_in.at[s, :], at_z(offset))))

    grams = []

    def stage_gram():
        gram[...] = lax.dot_general(
            scaled[...], hid[...], (((0,), (0,)), ((), ())), preferred_element_type=F32
        )
        mine = pl.ds(pl.multiple_of(k * FS, 64), FS)
        theirs = pl.ds(pl.multiple_of(other * FS, 64), FS)
        grams.append(remote(gram.at[theirs, :], gram_ref.at[k], sibling))
        grams.append(local(gram.at[mine, :], gram_ref.at[k]))

    halves = 2 * CHUNKS
    z_forward(1)
    stage_pick(0)
    z_forward(2)
    for n in range(halves + 5):
        if n < halves and n != 2:
            stage_spread(n)
        if n == 1:
            z_forward(3)
        if 1 <= n <= halves:
            stage_forward(n - 1)
        if n == 1:
            z_forward(4)
            stage_pick(ORDER[1])
        if n == 2:
            stage_pick(ORDER[2])
            stage_spread(n)
        if n == 4:
            stage_pick(ORDER[3])
        if 2 <= n < halves + 2:
            stage_hidden(n - 2)
        if 3 <= n < halves + 3:
            stage_hidden_forward(n - 3)
        if 4 <= n < halves + 4:
            stage_down(n - 4)
        if n == halves + 4:
            stage_gram()
        if n >= 6 and n % 2 == 0:
            stage_combine(ORDER[n // 2 - 3])

    total = part[pl.ds(0, TOK), :].astype(F32)
    for s, copy in parts:
        copy.wait_recv()
        total = total + part_in[s, :].astype(F32)
    out_ref[...] = total.astype(BF16)
    grams[0].wait_recv()
    grams[1].wait()
    for copy in sent:
        copy.wait_send()


def on_device(tokens, routes, route_weight, language, lang_weight, w_gate, w_up, w_down):
    langs = jnp.arange(lang_weight.shape[0], dtype=jnp.int32)
    cal = jnp.sum(jnp.where(language[None, :] == langs[:, None], lang_weight[:, None], 0.0), axis=0)
    rows = CHUNKS * ROWS
    anywhere = pl.BlockSpec(memory_space=pl.ANY)
    return pl.pallas_call(
        kernel,
        out_shape=(
            jax.ShapeDtypeStruct((TOK, DS), BF16),
            jax.ShapeDtypeStruct((2, FS, FF), F32),
        ),
        in_specs=[anywhere] * 7,
        out_specs=(pl.BlockSpec(memory_space=pltpu.VMEM), anywhere),
        scratch_shapes=[
            pltpu.VMEM((NZ * TOK, DS), BF16),
            pltpu.VMEM((8, TOK), jnp.int32),
            pltpu.VMEM((8, TOK), F32),
            pltpu.VMEM((1, TOK), F32),
            pltpu.VMEM((NZ, 24, TOK), F32),
            pltpu.VMEM((2, rows, DS), BF16),
            pltpu.VMEM((2, rows, DS), BF16),
            pltpu.VMEM((rows, TOK), BF16),
            pltpu.VMEM((rows, TOK), BF16),
            pltpu.VMEM((rows, D), BF16),
            pltpu.VMEM((2 * FC, D), BF16),
            pltpu.VMEM((2, FF, DS), BF16),
            pltpu.VMEM((rows, FC), BF16),
            pltpu.VMEM((rows, FC), BF16),
            pltpu.VMEM((rows, FF), BF16),
            pltpu.VMEM((2, rows, DS), BF16),
            pltpu.VMEM((2, rows, DS), BF16),
            pltpu.VMEM((CHUNKS, 2 * ROWS, 2 * TOK), BF16),
            pltpu.VMEM((CHUNKS, 2 * ROWS, 2 * TOK), BF16),
            pltpu.VMEM((NZ * TOK, DS), BF16),
            pltpu.VMEM((NZ * TOK, DS), BF16),
            pltpu.VMEM((FC, FF), F32),
            pltpu.SemaphoreType.DMA((NSEM,)),
            pltpu.SemaphoreType.DMA((NSEM,)),
            pltpu.SemaphoreType.DMA((40,)),
        ],
        compiler_params=pltpu.CompilerParams(
            collective_id=0, has_side_effects=True, vmem_limit_bytes=60 * 1024 * 1024
        ),
        name="routed_experts",
    )(tokens, routes.T, route_weight.T, cal[None, :], w_gate, w_up, w_down)


def solution(mesh):
    in_specs = (
        P("expert", "col"),
        P("expert", None),
        P("expert", None),
        P("expert"),
        P(),
        P("expert", "col", None),
        P("expert", "col", None),
        P("expert", None, "col"),
    )
    out_specs = (P("expert", "col"), P("expert", "col", None))
    return jax.shard_map(
        on_device, mesh=mesh, in_specs=in_specs, out_specs=out_specs, check_vma=False
    )
```
